32 devices in a mesh: patch: 8 (over z, y), rep: 4 (over x, core).
Axes of the slice: x: 2, y: 2, z: 4, core: 2. Of those that a mesh axis runs over, the one named last changes fastest.
Arguments:
- nodes: bfloat16 [4, 4096, 256], P('rep', 'patch'), may hold values from -6 to 6
- edges: bfloat16 [4, 12288, 256], P('rep', 'patch'), may hold values from -6 to 6
- edge_ends: int32 [12288, 2], P('patch'), may hold values from 0 to 543, as said below
- edge_count: int32 [8], P('patch'), may hold values from 768 to 1536, as said below
- send_rows: int32 [16, 16], P('patch'), may hold values from 0 to 511, as said below
- cotangent: bfloat16 [4, 4096, 256], P('rep', 'patch'), may hold values from -6 to 6
- edge_first: bfloat16 [768, 256], replicated, may hold values from -0.21875 to 0.21875
- edge_second: bfloat16 [256, 256], replicated, may hold values from -0.375 to 0.375
- node_first: bfloat16 [512, 256], replicated, may hold values from -0.25 to 0.25
- node_second: bfloat16 [256, 256], replicated, may hold values from -0.375 to 0.375
Outputs:
- new_nodes: bfloat16 [4, 4096, 256], P('rep', 'patch')
- grad_nodes: bfloat16 [4, 4096, 256], P('rep', 'patch')
- grad_edges: bfloat16 [4, 12288, 256], P('rep', 'patch')
- grad_edge_first: bfloat16 [768, 256], replicated
- grad_edge_second: bfloat16 [256, 256], replicated
- grad_node_first: bfloat16 [512, 256], replicated
- grad_node_second: bfloat16 [256, 256], replicated
The draws below stay inside these ranges and needn't reach their ends.
Inputs may be any that keep to these rules, and one draw needn't show every extreme that they name: `edge_ends`: in patch p's block, row j gives edge slot j: column 0 is a vertex of p; column 1 is a vertex of p, or 512 + h * 16 + s with h < 2, which names the vertex in slot s of row h of the send_rows block of patch (p + h + 1) mod 8. Padding slots hold ends of the same form. `edge_count`: live edge slots of each patch; slots at or beyond it are padding. Some patch has all 1536 live. `send_rows`: each patch's block has 2 rows of 16 distinct vertices of that patch, in its own numbering.
All inputs are finite; a program needn't handle non-finite values.
Results may differ from the reference program's by a relative error of at most 0.0084.
Values may be sent and summed in bfloat16 or wider, within the bound.
A program may use at most 64 MiB of HBM per device.

```python
import jax
import jax.numpy as jnp
from jax import lax

D = 256
V_DEV = 512
HOPS = 2
EDGE_DEV = 1536
SLOT = 16
SNAPS = 4
VERTS = 4096
EDGES = 12288
N_PATCH = 8


def draw_edge_ends(key, part):
    first_key, cut_key, choose_key, other_key = jax.random.split(jax.random.fold_in(key, 11), 4)
    first_end = jax.random.randint(first_key, (EDGES,), 0, V_DEV, dtype=jnp.int32)
    is_cut = jax.random.randint(cut_key, (EDGES,), 0, 4 * EDGE_DEV, dtype=jnp.int32) < 5 * HOPS * SLOT
    remote = V_DEV + jax.random.randint(choose_key, (EDGES,), 0, HOPS * SLOT, dtype=jnp.int32)
    nearby = (first_end + 1 + jax.random.randint(other_key, (EDGES,), 0, V_DEV - 1, dtype=jnp.int32)) % V_DEV
    second_end = jnp.where(is_cut, remote, nearby)
    return jnp.stack([first_end, second_end], axis=1).astype(jnp.int32)


def draw_edge_count(key, part):
    count_key, top_key = jax.random.split(jax.random.fold_in(key, 12))
    patches = EDGES // EDGE_DEV
    counts = jax.random.randint(count_key, (patches,), EDGE_DEV // 2, EDGE_DEV + 1, dtype=jnp.int32)
    fullest = jax.random.randint(top_key, (), 0, patches, dtype=jnp.int32)
    return jnp.where(jnp.arange(patches, dtype=jnp.int32) == fullest, EDGE_DEV, counts).astype(jnp.int32)


def pick_rows(one_key):
    return jax.random.permutation(one_key, V_DEV)[:SLOT]


def draw_send_rows(key, part):
    keys = jax.random.split(jax.random.fold_in(key, 13), EDGES // EDGE_DEV * HOPS)
    return jax.vmap(pick_rows)(keys).astype(jnp.int32)


def shard_levels(stream_key, shape, pieces, low, high):
    def one(dim, blocks):
        steps = jax.random.uniform(jax.random.fold_in(jax.random.fold_in(stream_key, 6), dim), (blocks,), jnp.float32, low / len(pieces), high / len(pieces))
        return jnp.repeat(jnp.exp(steps), shape[dim] // blocks).reshape((-1,) + (1,) * (len(shape) - dim - 1))

    level = one(*pieces[0])
    for cut in pieces[1:]:
        level = level * one(*cut)
    return level


def normal_values(key, shape, scale, limit, cuts=(), kind=jnp.bfloat16):
    loudness = shard_levels(key, shape, cuts, -0.22, 0.18) if cuts else 1.0
    result = jax.random.normal(key, shape, jnp.float32) * scale * loudness
    return jnp.minimum(jnp.maximum(result, -limit), limit).astype(kind)


def setup_inputs(seed: int = 0) -> dict:
    key_list = jax.random.split(jax.random.key(seed), 11)
    return {
        "nodes": normal_values(key_list[0], (SNAPS, VERTS, D), 1.0, 6.0, ((0, 4), (1, 8))),
        "edges": normal_values(key_list[1], (SNAPS, EDGES, D), 1.0, 6.0, ((0, 4), (1, 8))),
        "edge_ends": draw_edge_ends(jax.random.fold_in(key_list[10], 71), 0),
        "edge_count": draw_edge_count(jax.random.fold_in(key_list[10], 71), 0),
        "send_rows": draw_send_rows(jax.random.fold_in(key_list[10], 71), 0),
        "cotangent": normal_values(key_list[5], (SNAPS, VERTS, D), 1.0, 6.0, ((0, 4), (1, 8))),
        "edge_first": normal_values(key_list[6], (3 * D, D), (3 * D) ** -0.5, 0.21875),
        "edge_second": normal_values(key_list[7], (D, D), D ** -0.5, 0.375),
        "node_first": normal_values(key_list[8], (2 * D, D), (2 * D) ** -0.5, 0.25),
        "node_second": normal_values(key_list[9], (D, D), D ** -0.5, 0.375),
    }


EPS = 1e-05

def normalize(values):
    average = lax.optimization_barrier(jnp.mean(values, axis=-1, keepdims=True))
    centred = values - average
    inv_scale = lax.rsqrt(lax.optimization_barrier(jnp.mean(centred * centred, axis=-1, keepdims=True)) + EPS)
    return (centred * inv_scale, inv_scale)

def norm_back(upstream, normed, inv_scale):
    return inv_scale * (upstream - lax.optimization_barrier(jnp.mean(upstream, axis=-1, keepdims=True)) - normed * lax.optimization_barrier(jnp.mean(upstream * normed, axis=-1, keepdims=True)))

def silu_slope(pre):
    sigma = jax.nn.sigmoid(pre)
    return sigma * (1.0 + pre * (1.0 - sigma))

def matmul(left, right):
    return jnp.dot(left, right, preferred_element_type=jnp.float32)

def outer_sum(left, right):
    return lax.dot_general(left, right, (((0,), (0,)), ((), ())), preferred_element_type=jnp.float32)

def global_ends(edge_ends, edge_count, send_rows):
    owner = jnp.arange(EDGES, dtype=jnp.int32) // EDGE_DEV
    first_end = (owner * V_DEV + edge_ends[:, 0]).astype(jnp.int32)
    second = edge_ends[:, 1].astype(jnp.int32)
    remote = second - V_DEV
    offset = jnp.clip(remote // SLOT, 0, HOPS - 1).astype(jnp.int32)
    position = (remote % SLOT).astype(jnp.int32)
    partner = ((owner + offset + 1) % N_PATCH).astype(jnp.int32)
    far_row = partner * V_DEV + send_rows[partner * HOPS + offset, position]
    second_end = jnp.where(second < V_DEV, owner * V_DEV + second, far_row).astype(jnp.int32)
    slot_index = jnp.arange(EDGES, dtype=jnp.int32) % EDGE_DEV
    alive = (slot_index < edge_count[owner]).astype(jnp.float32)[:, None]
    return (first_end, second_end, alive)

def snapshot(node_rows, edge_rows, cot_rows, first_end, second_end, alive, edge_first, edge_second, node_first, node_second):
    features = node_rows.shape[1]
    first_rows = node_rows[first_end]
    second_rows = node_rows[second_end]
    edge_pre = matmul(edge_rows, edge_first[:features]) + matmul(first_rows, edge_first[features:2 * features]) + matmul(second_rows, edge_first[2 * features:])
    edge_hidden = jax.nn.silu(edge_pre).astype(jnp.bfloat16)
    edge_normed, edge_inv = normalize(matmul(edge_hidden, edge_second))
    new_edge = ((edge_rows.astype(jnp.float32) + edge_normed) * alive).astype(jnp.bfloat16)
    new_wide = lax.optimization_barrier(new_edge).astype(jnp.float32)
    verts = node_rows.shape[0]
    aggregate = (jax.ops.segment_sum(new_wide, first_end, verts) + jax.ops.segment_sum(new_wide, second_end, verts)).astype(jnp.bfloat16)
    node_pre = matmul(node_rows, node_first[:features]) + matmul(aggregate, node_first[features:])
    node_hidden = jax.nn.silu(node_pre).astype(jnp.bfloat16)
    node_normed, node_inv = normalize(matmul(node_hidden, node_second))
    new_nodes = (node_rows.astype(jnp.float32) + node_normed).astype(jnp.bfloat16)
    cot_wide = cot_rows.astype(jnp.float32)
    d_node_out = norm_back(cot_wide, node_normed, node_inv).astype(jnp.bfloat16)
    grad_ns = outer_sum(node_hidden, d_node_out)
    d_node_pre = (matmul(d_node_out, node_second.T) * silu_slope(node_pre)).astype(jnp.bfloat16)
    grad_nf = jnp.concatenate([outer_sum(node_rows, d_node_pre), outer_sum(aggregate, d_node_pre)], axis=0)
    d_direct = matmul(d_node_pre, node_first[:features].T)
    d_aggregate = matmul(d_node_pre, node_first[features:].T).astype(jnp.bfloat16)
    d_new_edge = alive * (d_aggregate[first_end].astype(jnp.float32) + d_aggregate[second_end].astype(jnp.float32))
    d_edge_out = norm_back(d_new_edge, edge_normed, edge_inv).astype(jnp.bfloat16)
    grad_es = outer_sum(edge_hidden, d_edge_out)
    d_edge_pre = (matmul(d_edge_out, edge_second.T) * silu_slope(edge_pre)).astype(jnp.bfloat16)
    grad_ef = jnp.concatenate([outer_sum(edge_rows, d_edge_pre), outer_sum(first_rows, d_edge_pre), outer_sum(second_rows, d_edge_pre)], axis=0)
    grad_edges = (d_new_edge + matmul(d_edge_pre, edge_first[:features].T)).astype(jnp.bfloat16)
    d_first_end = matmul(d_edge_pre, edge_first[features:2 * features].T)
    d_second_end = matmul(d_edge_pre, edge_first[2 * features:].T)
    grad_nodes = (cot_wide + d_direct + jax.ops.segment_sum(d_first_end, first_end, verts) + jax.ops.segment_sum(d_second_end, second_end, verts)).astype(jnp.bfloat16)
    return (new_nodes, grad_nodes, grad_edges, grad_ef, grad_es, grad_nf, grad_ns)

def reference(nodes, edges, edge_ends, edge_count, send_rows, cotangent, edge_first, edge_second, node_first, node_second):
    first_end, second_end, alive = global_ends(edge_ends, edge_count, send_rows)

    def one_snapshot(inputs):
        return snapshot(inputs[0], inputs[1], inputs[2], first_end, second_end, alive, edge_first, edge_second, node_first, node_second)
    results = lax.map(one_snapshot, (nodes, edges, cotangent))
    new_nodes, grad_nodes, grad_edges = (results[0], results[1], results[2])
    summed = [lax.optimization_barrier(jnp.sum(part, axis=0)).astype(jnp.bfloat16) for part in results[3:]]
    return (new_nodes, grad_nodes, grad_edges, summed[0], summed[1], summed[2], summed[3])
```

```python
import functools

import jax
import jax.numpy as jnp
from jax import lax
from jax.experimental import pallas as pl
from jax.experimental.pallas import tpu as pltpu
from jax.sharding import PartitionSpec as P

EPS = 1e-05
MESH = pl.DeviceIdType.MESH
F32 = jnp.float32
BF16 = jnp.bfloat16
LANES = 128
PACK = 16


def mm(left, right):
    return jnp.dot(left, right, preferred_element_type=F32)


def mm_nt(left, right):
    return lax.dot_general(left, right, (((1,), (1,)), ((), ())), preferred_element_type=F32)


def mm_tn(left, right):
    return lax.dot_general(left, right, (((0,), (0,)), ((), ())), preferred_element_type=F32)


def normalize(values):
    average = jnp.mean(values, axis=-1, keepdims=True)
    centred = values - average
    inv_scale = lax.rsqrt(jnp.mean(centred * centred, axis=-1, keepdims=True) + EPS)
    return centred * inv_scale, inv_scale


def norm_back(upstream, normed, inv_scale):
    return inv_scale * (
        upstream
        - jnp.mean(upstream, axis=-1, keepdims=True)
        - normed * jnp.mean(upstream * normed, axis=-1, keepdims=True)
    )


def ones_where(mask):
    return jnp.where(mask, 1.0, 0.0).astype(F32)


def as_column(row):
    n = row.shape[1]
    eye = lax.broadcasted_iota(jnp.int32, (n, n), 0) == lax.broadcasted_iota(jnp.int32, (n, n), 1)
    wide = jnp.broadcast_to(row.astype(F32), (n, n))
    return jnp.sum(jnp.where(eye, wide, 0.0), axis=1, keepdims=True)


def tile_of(total, wanted):
    while total % wanted:
        wanted //= 2
    return wanted


def body(sizes, *refs):
    fused, patches, reps, group = sizes
    (nodes, edges, ends_t, count, send, cot, ef, es, nf, ns) = refs[:10]
    new_nodes, g_nodes, g_edges = refs[10:13]
    rest = refs[13:]
    if fused:
        g_ef, g_es, g_nf, g_ns, acc = rest[:5]
        rest = rest[5:]
    else:
        acc = rest[0]
        rest = rest[1:]
    (cols, pick, tab1, tab2, slope, normed, inv, hidden, msg, halo_src, halo_dst,
     wide, node_pre, node_hidden, d_node_out, d_node_pre, d_tab, sums1, sums2,
     seam_send, seam_recv) = rest[:21]
    rest = rest[21:]
    if fused:
        pair_out, pair_in, chip_sum, ring_in, final, final_other, ar_send, ar_recv = rest

    verts, width = nodes.shape
    slots = edges.shape[0]
    hops, slot = send.shape
    seam = hops * slot
    table = tab2.shape[0]
    tile = tile_of(slots, 256)
    vtile = tile_of(verts, 256)
    me_p = lax.axis_index("patch")
    me_r = lax.axis_index("rep")

    barrier = pltpu.get_barrier_semaphore()
    if fused:
        chips_r = reps // 2
        core = lax.rem(me_r, 2)
        partner = me_r + 1 - 2 * core
        me_g = me_p * chips_r + me_r // 2

        def group_device(k):
            peer = lax.rem(me_g + k, group)
            return peer, {"patch": peer // chips_r, "rep": lax.rem(peer, chips_r) * 2 + core}

        @pl.loop(1, group)
        def _(k):
            _, dev = group_device(k)
            pl.semaphore_signal(barrier, inc=1, device_id=dev, device_id_type=MESH)

        pl.semaphore_signal(barrier, inc=1, device_id={"rep": partner}, device_id_type=MESH)
        greeted = group
    else:
        for step in range(1, hops + 1):
            for other in (lax.rem(me_p + step, patches), lax.rem(me_p + patches - step, patches)):
                pl.semaphore_signal(
                    barrier, inc=1, device_id={"patch": other}, device_id_type=MESH
                )
        greeted = 2 * hops

    def seam_copies(stage):
        down = stage % 2 == 0
        made = []
        for h in range(hops):
            step = patches - h - 1 if down else h + 1
            made.append(
                pltpu.make_async_remote_copy(
                    src_ref=halo_src.at[stage, h],
                    dst_ref=halo_dst.at[stage, h],
                    send_sem=seam_send.at[stage, h],
                    recv_sem=seam_recv.at[stage, h],
                    device_id={"patch": lax.rem(me_p + step, patches)},
                    device_id_type=MESH,
                )
            )
        return made

    def seam_start(stage, values):
        for h in range(hops):
            halo_src[stage, h] = values[h * slot : (h + 1) * slot].astype(BF16)
        for copy in seam_copies(stage):
            copy.start()

    def seam_wait(stage):
        for copy in seam_copies(stage):
            copy.wait()
        return jnp.concatenate([halo_dst[stage, h] for h in range(hops)], axis=0)

    class Bucket:
        def __init__(self, index, row, rows):
            self.index, self.row, self.rows = index, row, rows
            self.first = row // PACK
            self.blocks = rows // PACK
            if fused:
                self.own = self.blocks // group

        def pair(self, phase, src, dst):
            span = pl.ds(self.first, self.blocks)
            return pltpu.make_async_remote_copy(
                src_ref=src.at[span],
                dst_ref=dst.at[span],
                send_sem=ar_send.at[self.index, phase, 0],
                recv_sem=ar_recv.at[self.index, phase, 0],
                device_id={"rep": partner},
                device_id_type=MESH,
            )

        def scatter_copy(self, k):
            peer, dev = group_device(k)
            return pltpu.make_async_remote_copy(
                src_ref=chip_sum.at[pl.ds(self.first + peer * self.own, self.own)],
                dst_ref=ring_in.at[pl.ds(self.first + k * self.own, self.own)],
                send_sem=ar_send.at[self.index, 1, k],
                recv_sem=ar_recv.at[self.index, 1, k],
                device_id=dev,
                device_id_type=MESH,
            )

        def gather_copy(self, k):
            _, dev = group_device(k)
            mine = pl.ds(self.first + me_g * self.own, self.own)
            return pltpu.make_async_remote_copy(
                src_ref=final.at[mine],
                dst_ref=final.at[mine],
                send_sem=ar_send.at[self.index, 2, k],
                recv_sem=ar_recv.at[self.index, 2, k],
                device_id=dev,
                device_id_type=MESH,
            )

        def halves(self):
            low = acc[self.row : self.row + self.rows, :LANES]
            high = acc[self.row : self.row + self.rows, LANES:]
            return low, high

        def start_pair(self):
            if not fused:
                return
            low, high = self.halves()
            other = jnp.where(core == 0, high, low)
            pair_out[self.first : self.first + self.blocks] = other.astype(BF16).reshape(
                self.blocks, PACK, LANES
            )
            self.pair(0, pair_out, pair_in).start()

        def start_scatter(self):
            if not fused:
                return
            self.pair(0, pair_out, pair_in).wait()
            low, high = self.halves()
            mine = jnp.where(core == 0, low, high).reshape(self.blocks, PACK, LANES)
            got = pair_in[self.first : self.first + self.blocks].astype(F32)
            chip_sum[self.first : self.first + self.blocks] = (mine + got).astype(BF16)

            @pl.loop(1, group)
            def _(k):
                self.scatter_copy(k).start()

        def start_gather(self):
            if not fused:
                return

            @pl.loop(1, group)
            def _(k):
                self.scatter_copy(k).wait()

            mine = pl.ds(self.first + me_g * self.own, self.own)
            total = chip_sum[mine].astype(F32)
            for k in range(1, group):
                at = self.first + k * self.own
                total = total + ring_in[at : at + self.own].astype(F32)
            final[mine] = total.astype(BF16)

            @pl.loop(1, group)
            def _(k):
                self.gather_copy(k).start()

        def start_share(self):
            if not fused:
                return

            @pl.loop(1, group)
            def _(k):
                self.gather_copy(k).wait()

            self.pair(3, final, final_other).start()

        def finish(self, targets):
            if not fused:
                return
            self.pair(3, final, final_other).wait()
            at = self.first
            for ref, row, rows in targets:
                n = rows // PACK
                a = final[at : at + n].reshape(rows, LANES)
                b = final_other[at : at + n].reshape(rows, LANES)
                ref[row : row + rows, :LANES] = jnp.where(core == 0, a, b)
                ref[row : row + rows, LANES:] = jnp.where(core == 0, b, a)
                at += n

    node_bucket = Bucket(0, 0, 3 * width)
    mid_bucket = Bucket(1, 3 * width, 2 * width)
    end_bucket = Bucket(2, 5 * width, 2 * width)

    lane_v = lax.broadcasted_iota(jnp.int32, (slot, verts), 1).astype(F32)
    for h in range(hops):
        chosen = as_column(send[h : h + 1, :])
        pick[h * slot : (h + 1) * slot, :] = ones_where(lane_v == chosen).astype(BF16)
    outgoing = mm(pick[...], nodes[...])
    pl.semaphore_wait(barrier, greeted)
    seam_start(0, outgoing)

    @pl.loop(0, slots // LANES)
    def _(j):
        at = pl.ds(pl.multiple_of(j * LANES, LANES), LANES)
        for end in range(2):
            column = as_column(ends_t[end : end + 1, at])
            cols[end, at, :] = jnp.broadcast_to(column, (LANES, LANES)).astype(jnp.int32)

    tab1[...] = mm(nodes[...], ef[width : 2 * width, :]).astype(BF16)
    tab2[0:verts, :] = mm(nodes[...], ef[2 * width :, :]).astype(BF16)
    if table > verts + seam:
        tab2[verts + seam :, :] = jnp.zeros((table - verts - seam, width), BF16)
        d_tab[verts + seam :, :] = jnp.zeros((table - verts - seam, width), BF16)
    halo = seam_wait(0)
    tab2[verts : verts + seam, :] = mm(halo, ef[2 * width :, :]).astype(BF16)

    lane_e = lax.broadcasted_iota(jnp.int32, (tile, LANES), 1)

    def ends_hot(column, size):
        return jnp.concatenate(
            [ones_where(column == lane_e + k) for k in range(0, size, LANES)], axis=1
        )

    def alive_of(start):
        at = lax.broadcasted_iota(jnp.int32, (tile, 1), 0) + start
        return ones_where(at < count[0])

    @pl.loop(0, slots // tile)
    def _(i):
        start = pl.multiple_of(i * tile, tile)
        at = pl.ds(start, tile)
        first = ends_hot(cols[0, at, :], verts).astype(BF16)
        second = ends_hot(cols[1, at, :], table).astype(BF16)
        rows = edges[at, :]
        pre = mm(rows, ef[:width, :]) + mm(first, tab1[...]) + mm(second, tab2[...])
        sigma = jax.nn.sigmoid(pre)
        hid = (pre * sigma).astype(BF16)
        slope[at, :] = sigma * (1.0 + pre * (1.0 - sigma))
        hidden[at, :] = hid
        out, scale = normalize(mm(hid, es[...]))
        normed[at, :] = out
        inv[at, :] = scale
        msg[at, :] = (alive_of(start) * (rows.astype(F32) + out)).astype(BF16)

    sub_v = lax.broadcasted_iota(jnp.int32, (LANES, slots), 0)

    def hot_rows(end, start):
        return ones_where(ends_t[end : end + 1, :] == sub_v + start)

    seam_hot = hot_rows(1, verts).astype(BF16)
    seam_start(1, mm(seam_hot, msg[...])[:seam])

    @pl.loop(0, verts // LANES)
    def _(i):
        start = pl.multiple_of(i * LANES, LANES)
        both = (hot_rows(0, start) + hot_rows(1, start)).astype(BF16)
        wide[pl.ds(start, LANES), :] = mm(both, msg[...])

    node_pre[...] = mm(nodes[...], nf[:width, :])
    returned = seam_wait(1)
    wide[...] += mm_tn(pick[...], returned)
    aggregate = tab1
    aggregate[...] = wide[...].astype(BF16)

    @pl.loop(0, verts // vtile)
    def _(i):
        at = pl.ds(pl.multiple_of(i * vtile, vtile), vtile)
        pre = node_pre[at, :] + mm(aggregate[at, :], nf[width:, :])
        sigma = jax.nn.sigmoid(pre)
        hid = (pre * sigma).astype(BF16)
        node_hidden[at, :] = hid
        out, scale = normalize(mm(hid, ns[...]))
        new_nodes[at, :] = (nodes[at, :].astype(F32) + out).astype(BF16)
        d_out = norm_back(cot[at, :].astype(F32), out, scale).astype(BF16)
        d_node_out[at, :] = d_out
        d_pre = (mm_nt(d_out, ns[...]) * (sigma * (1.0 + pre * (1.0 - sigma)))).astype(BF16)
        d_node_pre[at, :] = d_pre
        d_tab[at, :] = mm_nt(d_pre, nf[width:, :]).astype(BF16)

    seam_start(2, mm(pick[...], d_tab[0:verts, :]))
    acc[0:width, :] = mm_tn(node_hidden[...], d_node_out[...])
    acc[width : 2 * width, :] = mm_tn(nodes[...], d_node_pre[...])
    acc[2 * width : 3 * width, :] = mm_tn(aggregate[...], d_node_pre[...])
    node_bucket.start_pair()
    wide[...] = cot[...].astype(F32) + mm_nt(d_node_pre[...], nf[:width, :])
    acc[3 * width : 5 * width, :] = jnp.zeros((2 * width, width), F32)
    d_tab[verts : verts + seam, :] = seam_wait(2)
    node_bucket.start_scatter()

    d_edge_pre = msg

    @pl.loop(0, slots // tile)
    def _(i):
        start = pl.multiple_of(i * tile, tile)
        at = pl.ds(start, tile)
        both = (
            jnp.concatenate(
                [ends_hot(cols[0, at, :], verts), jnp.zeros((tile, table - verts), F32)], axis=1
            )
            + ends_hot(cols[1, at, :], table)
        ).astype(BF16)
        d_new = alive_of(start) * mm(both, d_tab[...])
        d_out = norm_back(d_new, normed[at, :], inv[at, :]).astype(BF16)
        d_pre = (mm_nt(d_out, es[...]) * slope[at, :]).astype(BF16)
        d_edge_pre[at, :] = d_pre
        g_edges[at, :] = (d_new + mm_nt(d_pre, ef[:width, :])).astype(BF16)
        acc[3 * width : 4 * width, :] += mm_tn(hidden[at, :], d_out)
        acc[4 * width : 5 * width, :] += mm_tn(edges[at, :], d_pre)

    mid_bucket.start_pair()
    seam_sums = mm(seam_hot, d_edge_pre[...])[:seam].astype(BF16)
    seam_start(3, seam_sums)
    node_bucket.start_gather()

    @pl.loop(0, verts // LANES)
    def _(i):
        start = pl.multiple_of(i * LANES, LANES)
        at = pl.ds(start, LANES)
        sums1[at, :] = mm(hot_rows(0, start).astype(BF16), d_edge_pre[...]).astype(BF16)
        sums2[at, :] = mm(hot_rows(1, start).astype(BF16), d_edge_pre[...])

    mid_bucket.start_scatter()
    acc[5 * width : 6 * width, :] = mm_tn(nodes[...], sums1[...])
    acc[6 * width : 7 * width, :] = mm_tn(nodes[...], sums2[...].astype(BF16)) + mm_tn(
        halo, seam_sums
    )
    end_bucket.start_pair()
    part = wide[...] + mm_nt(sums1[...], ef[width : 2 * width, :])
    end_bucket.start_scatter()
    returned = seam_wait(3)
    second = (sums2[...] + mm_tn(pick[...], returned)).astype(BF16)
    g_nodes[...] = (part + mm_nt(second, ef[2 * width :, :])).astype(BF16)
    mid_bucket.start_gather()
    node_bucket.start_share()
    end_bucket.start_gather()
    mid_bucket.start_share()
    if fused:
        node_bucket.finish([(g_ns, 0, width), (g_nf, 0, 2 * width)])
    end_bucket.start_share()
    if fused:
        mid_bucket.finish([(g_es, 0, width), (g_ef, 0, width)])
        end_bucket.finish([(g_ef, width, 2 * width)])


def local(sizes, nodes, edges, edge_ends, edge_count, send_rows, cotangent, ef, es, nf, ns):
    fused, patches, reps, group = sizes
    verts, width = nodes.shape[1:]
    slots = edges.shape[1]
    hops, slot = send_rows.shape
    seam = hops * slot
    table = verts + -(-seam // LANES) * LANES
    rows = ef.shape[0] + es.shape[0] + nf.shape[0] + ns.shape[0]
    vmem = pl.BlockSpec(memory_space=pltpu.VMEM)
    smem = pl.BlockSpec(memory_space=pltpu.SMEM)

    def like(shape, kind=BF16):
        return jax.ShapeDtypeStruct(shape, kind)

    outs = [like((verts, width)), like((verts, width)), like((slots, width))]
    if fused:
        outs += [like(ef.shape), like(es.shape), like(nf.shape), like(ns.shape)]
    else:
        outs += [like((rows, width), F32)]
    scratch = [pltpu.VMEM((rows, width), F32)] if fused else []
    scratch += [
        pltpu.VMEM((2, slots, LANES), jnp.int32),
        pltpu.VMEM((seam, verts), BF16),
        pltpu.VMEM((verts, width), BF16),
        pltpu.VMEM((table, width), BF16),
        pltpu.VMEM((slots, width), F32),
        pltpu.VMEM((slots, width), F32),
        pltpu.VMEM((slots, 1), F32),
        pltpu.VMEM((slots, width), BF16),
        pltpu.VMEM((slots, width), BF16),
        pltpu.VMEM((4, hops, slot, width), BF16),
        pltpu.VMEM((4, hops, slot, width), BF16),
        pltpu.VMEM((verts, width), F32),
        pltpu.VMEM((verts, width), F32),
        pltpu.VMEM((verts, width), BF16),
        pltpu.VMEM((verts, width), BF16),
        pltpu.VMEM((verts, width), BF16),
        pltpu.VMEM((table, width), BF16),
        pltpu.VMEM((verts, width), BF16),
        pltpu.VMEM((verts, width), F32),
        pltpu.SemaphoreType.DMA((4, hops)),
        pltpu.SemaphoreType.DMA((4, hops)),
    ]
    if fused:
        scratch += [pltpu.VMEM((rows // PACK, PACK, LANES), BF16)] * 6
        scratch += [pltpu.SemaphoreType.DMA((3, 4, group))] * 2
    got = pl.pallas_call(
        functools.partial(body, sizes),
        out_shape=outs,
        in_specs=[vmem, vmem, vmem, smem, vmem, vmem, vmem, vmem, vmem, vmem],
        out_specs=[vmem] * len(outs),
        scratch_shapes=scratch,
        compiler_params=pltpu.CompilerParams(
            collective_id=0, has_side_effects=True, vmem_limit_bytes=48 * 2**20
        ),
        name="message_layer",
    )(nodes[0], edges[0], edge_ends.T, edge_count, send_rows, cotangent[0], ef, es, nf, ns)
    new_nodes, g_nodes, g_edges = got[:3]
    if fused:
        g_ef, g_es, g_nf, g_ns = got[3:]
    else:
        total = lax.psum(got[3], ("patch", "rep")).astype(BF16)
        g_ns = total[:width]
        g_nf = total[width : 3 * width]
        g_es = total[3 * width : 4 * width]
        g_ef = total[4 * width :]
    return new_nodes[None], g_nodes[None], g_edges[None], g_ef, g_es, g_nf, g_ns


def solution(mesh):
    patches, reps = mesh.shape["patch"], mesh.shape["rep"]
    group = patches * reps // 2
    fused = reps % 2 == 0 and (2 * LANES) % (PACK * group) == 0
    sizes = (fused, patches, reps, group)
    rows = P("rep", "patch", None)
    placed = (rows, rows, P("patch", None), P("patch"), P("patch", None), rows, P(), P(), P(), P())
    return jax.shard_map(
        functools.partial(local, sizes),
        mesh=mesh,
        in_specs=placed,
        out_specs=(rows, rows, rows, P(), P(), P(), P()),
        check_vma=False,
    )
```

```python
import functools

import jax
import jax.numpy as jnp
from jax import lax
from jax.experimental import pallas as pl
from jax.experimental.pallas import tpu as pltpu
from jax.sharding import PartitionSpec as P

EPS = 1e-05
MESH = pl.DeviceIdType.MESH
F32 = jnp.float32
BF16 = jnp.bfloat16
LANES = 128
PACK = 16


def mm(left, right):
    return jnp.dot(left, right, preferred_element_type=F32)


def mm_nt(left, right):
    return lax.dot_general(left, right, (((1,), (1,)), ((), ())), preferred_element_type=F32)


def mm_tn(left, right):
    return lax.dot_general(left, right, (((0,), (0,)), ((), ())), preferred_element_type=F32)


def normalize(values):
    average = jnp.mean(values, axis=-1, keepdims=True)
    centred = values - average
    inv_scale = lax.rsqrt(jnp.mean(centred * centred, axis=-1, keepdims=True) + EPS)
    return centred * inv_scale, inv_scale


def norm_back(upstream, normed, inv_scale):
    return inv_scale * (
        upstream
        - jnp.mean(upstream, axis=-1, keepdims=True)
        - normed * jnp.mean(upstream * normed, axis=-1, keepdims=True)
    )


def ones_where(mask):
    return jnp.where(mask, 1.0, 0.0).astype(F32)


def as_column(row):
    n = row.shape[1]
    eye = lax.broadcasted_iota(jnp.int32, (n, n), 0) == lax.broadcasted_iota(jnp.int32, (n, n), 1)
    wide = jnp.broadcast_to(row.astype(F32), (n, n))
    return jnp.sum(jnp.where(eye, wide, 0.0), axis=1, keepdims=True)


def tile_of(total, wanted):
    while total % wanted:
        wanted //= 2
    return wanted


def body(sizes, *refs):
    fused, patches, reps, group = sizes
    count = refs[3]
    held = refs[:3] + refs[4:10]
    new_nodes, g_nodes, g_edges = refs[10:13]
    rest = refs[13:]
    if fused:
        g_ef, g_es, g_nf, g_ns, acc = rest[:5]
        rest = rest[5:]
    else:
        acc = rest[0]
        rest = rest[1:]
    (cols, pick, tab1, tab2, slope, normed, inv, hidden, msg, halo_src, halo_dst,
     wide, node_pre, node_hidden, d_node_out, d_node_pre, d_tab, sums1, sums2,
     seam_send, seam_recv) = rest[:21]
    (nodes, edges, ends_t, send, cot, ef, es, nf, ns) = rest[21:30]
    loads = rest[30]
    rest = rest[31:]
    if fused:
        pair_out, pair_in, chip_sum, ring_in, final, final_other, ar_send, ar_recv = rest

    verts, width = nodes.shape
    slots = edges.shape[0]
    hops, slot = send.shape
    seam = hops * slot
    table = tab2.shape[0]
    tile = tile_of(slots, 256)
    vtile = tile_of(verts, 256)
    me_p = lax.axis_index("patch")
    me_r = lax.axis_index("rep")

    loaded = [
        pltpu.make_async_copy(src, dst, loads.at[i])
        for i, (src, dst) in enumerate(
            zip(held, (nodes, edges, ends_t, send, cot, ef, es, nf, ns), strict=True)
        )
    ]
    for i in (3, 0, 2, 5, 1, 6, 7, 8, 4):
        loaded[i].start()

    barrier = pltpu.get_barrier_semaphore()
    if fused:
        chips_r = reps // 2
        core = lax.rem(me_r, 2)
        partner = me_r + 1 - 2 * core
        me_g = me_p * chips_r + me_r // 2

        def group_device(k):
            peer = lax.rem(me_g + k, group)
            return peer, {"patch": peer // chips_r, "rep": lax.rem(peer, chips_r) * 2 + core}

        @pl.loop(1, group)
        def _(k):
            _, dev = group_device(k)
            pl.semaphore_signal(barrier, inc=1, device_id=dev, device_id_type=MESH)

        pl.semaphore_signal(barrier, inc=1, device_id={"rep": partner}, device_id_type=MESH)
        greeted = group
    else:
        for step in range(1, hops + 1):
            for other in (lax.rem(me_p + step, patches), lax.rem(me_p + patches - step, patches)):
                pl.semaphore_signal(
                    barrier, inc=1, device_id={"patch": other}, device_id_type=MESH
                )
        greeted = 2 * hops

    def seam_copies(stage):
        down = stage % 2 == 0
        made = []
        for h in range(hops):
            step = patches - h - 1 if down else h + 1
            made.append(
                pltpu.make_async_remote_copy(
                    src_ref=halo_src.at[stage, h],
                    dst_ref=halo_dst.at[stage, h],
                    send_sem=seam_send.at[stage, h],
                    recv_sem=seam_recv.at[stage, h],
                    device_id={"patch": lax.rem(me_p + step, patches)},
                    device_id_type=MESH,
                )
            )
        return made

    def seam_start(stage, values):
        for h in range(hops):
            halo_src[stage, h] = values[h * slot : (h + 1) * slot].astype(BF16)
        for copy in seam_copies(stage):
            copy.start()

    def seam_wait(stage):
        for copy in seam_copies(stage):
            copy.wait()
        return jnp.concatenate([halo_dst[stage, h] for h in range(hops)], axis=0)

    class Bucket:
        def __init__(self, index, row, rows):
            self.index, self.row, self.rows = index, row, rows
            self.first = row // PACK
            self.blocks = rows // PACK
            if fused:
                self.own = self.blocks // group

        def pair(self, phase, src, dst):
            span = pl.ds(self.first, self.blocks)
            return pltpu.make_async_remote_copy(
                src_ref=src.at[span],
                dst_ref=dst.at[span],
                send_sem=ar_send.at[self.index, phase, 0],
                recv_sem=ar_recv.at[self.index, phase, 0],
                device_id={"rep": partner},
                device_id_type=MESH,
            )

        def scatter_copy(self, k):
            peer, dev = group_device(k)
            return pltpu.make_async_remote_copy(
                src_ref=chip_sum.at[pl.ds(self.first + peer * self.own, self.own)],
                dst_ref=ring_in.at[pl.ds(self.first + k * self.own, self.own)],
                send_sem=ar_send.at[self.index, 1, k],
                recv_sem=ar_recv.at[self.index, 1, k],
                device_id=dev,
                device_id_type=MESH,
            )

        def gather_copy(self, k):
            _, dev = group_device(k)
            mine = pl.ds(self.first + me_g * self.own, self.own)
            return pltpu.make_async_remote_copy(
                src_ref=final.at[mine],
                dst_ref=final.at[mine],
                send_sem=ar_send.at[self.index, 2, k],
                recv_sem=ar_recv.at[self.index, 2, k],
                device_id=dev,
                device_id_type=MESH,
            )

        def halves(self):
            low = acc[self.row : self.row + self.rows, :LANES]
            high = acc[self.row : self.row + self.rows, LANES:]
            return low, high

        def start_pair(self):
            if not fused:
                return
            low, high = self.halves()
            other = jnp.where(core == 0, high, low)
            pair_out[self.first : self.first + self.blocks] = other.astype(BF16).reshape(
                self.blocks, PACK, LANES
            )
            self.pair(0, pair_out, pair_in).start()

        def start_scatter(self):
            if not fused:
                return
            self.pair(0, pair_out, pair_in).wait()
            low, high = self.halves()
            mine = jnp.where(core == 0, low, high).reshape(self.blocks, PACK, LANES)
            got = pair_in[self.first : self.first + self.blocks].astype(F32)
            chip_sum[self.first : self.first + self.blocks] = (mine + got).astype(BF16)

            @pl.loop(1, group)
            def _(k):
                self.scatter_copy(k).start()

        def start_gather(self):
            if not fused:
                return

            @pl.loop(1, group)
            def _(k):
                self.scatter_copy(k).wait()

            mine = pl.ds(self.first + me_g * self.own, self.own)
            total = chip_sum[mine].astype(F32)
            for k in range(1, group):
                at = self.first + k * self.own
                total = total + ring_in[at : at + self.own].astype(F32)
            final[mine] = total.astype(BF16)

            @pl.loop(1, group)
            def _(k):
                self.gather_copy(k).start()

        def start_share(self):
            if not fused:
                return

            @pl.loop(1, group)
            def _(k):
                self.gather_copy(k).wait()

            self.pair(3, final, final_other).start()

        def finish(self, targets):
            if not fused:
                return
            self.pair(3, final, final_other).wait()
            at = self.first
            for ref, row, rows in targets:
                n = rows // PACK
                a = final[at : at + n].reshape(rows, LANES)
                b = final_other[at : at + n].reshape(rows, LANES)
                ref[row : row + rows, :LANES] = jnp.where(core == 0, a, b)
                ref[row : row + rows, LANES:] = jnp.where(core == 0, b, a)
                at += n

    node_bucket = Bucket(0, 0, 3 * width)
    mid_bucket = Bucket(1, 3 * width, 2 * width)
    end_bucket = Bucket(2, 5 * width, 2 * width)

    loaded[3].wait()
    loaded[0].wait()
    lane_v = lax.broadcasted_iota(jnp.int32, (slot, verts), 1).astype(F32)
    for h in range(hops):
        chosen = as_column(send[h : h + 1, :])
        pick[h * slot : (h + 1) * slot, :] = ones_where(lane_v == chosen).astype(BF16)
    outgoing = mm(pick[...], nodes[...])
    pl.semaphore_wait(barrier, greeted)
    seam_start(0, outgoing)

    loaded[2].wait()
    @pl.loop(0, slots // LANES)
    def _(j):
        at = pl.ds(pl.multiple_of(j * LANES, LANES), LANES)
        for end in range(2):
            column = as_column(ends_t[end : end + 1, at])
            cols[end, at, :] = jnp.broadcast_to(column, (LANES, LANES)).astype(jnp.int32)

    loaded[5].wait()
    tab1[...] = mm(nodes[...], ef[width : 2 * width, :]).astype(BF16)
    tab2[0:verts, :] = mm(nodes[...], ef[2 * width :, :]).astype(BF16)
    if table > verts + seam:
        tab2[verts + seam :, :] = jnp.zeros((table - verts - seam, width), BF16)
        d_tab[verts + seam :, :] = jnp.zeros((table - verts - seam, width), BF16)
    loaded[1].wait()
    loaded[6].wait()
    halo = seam_wait(0)
    tab2[verts : verts + seam, :] = mm(halo, ef[2 * width :, :]).astype(BF16)

    lane_e = lax.broadcasted_iota(jnp.int32, (tile, LANES), 1)

    def ends_hot(column, size):
        return jnp.concatenate(
            [ones_where(column == lane_e + k) for k in range(0, size, LANES)], axis=1
        )

    def alive_of(start):
        at = lax.broadcasted_iota(jnp.int32, (tile, 1), 0) + start
        return ones_where(at < count[0])

    @pl.loop(0, slots // tile)
    def _(i):
        start = pl.multiple_of(i * tile, tile)
        at = pl.ds(start, tile)
        first = ends_hot(cols[0, at, :], verts).astype(BF16)
        second = ends_hot(cols[1, at, :], table).astype(BF16)
        rows = edges[at, :]
        pre = mm(rows, ef[:width, :]) + mm(first, tab1[...]) + mm(second, tab2[...])
        sigma = jax.nn.sigmoid(pre)
        hid = (pre * sigma).astype(BF16)
        slope[at, :] = sigma * (1.0 + pre * (1.0 - sigma))
        hidden[at, :] = hid
        out, scale = normalize(mm(hid, es[...]))
        normed[at, :] = out
        inv[at, :] = scale
        msg[at, :] = (alive_of(start) * (rows.astype(F32) + out)).astype(BF16)

    sub_v = lax.broadcasted_iota(jnp.int32, (LANES, slots), 0)

    def hot_rows(end, start):
        return ones_where(ends_t[end : end + 1, :] == sub_v + start)

    seam_hot = hot_rows(1, verts).astype(BF16)
    seam_start(1, mm(seam_hot, msg[...])[:seam])

    @pl.loop(0, verts // LANES)
    def _(i):
        start = pl.multiple_of(i * LANES, LANES)
        both = (hot_rows(0, start) + hot_rows(1, start)).astype(BF16)
        wide[pl.ds(start, LANES), :] = mm(both, msg[...])

    for i in (7, 8, 4):
        loaded[i].wait()
    node_pre[...] = mm(nodes[...], nf[:width, :])
    returned = seam_wait(1)
    wide[...] += mm_tn(pick[...], returned)
    aggregate = tab1
    aggregate[...] = wide[...].astype(BF16)

    @pl.loop(0, verts // vtile)
    def _(i):
        at = pl.ds(pl.multiple_of(i * vtile, vtile), vtile)
        pre = node_pre[at, :] + mm(aggregate[at, :], nf[width:, :])
        sigma = jax.nn.sigmoid(pre)
        hid = (pre * sigma).astype(BF16)
        node_hidden[at, :] = hid
        out, scale = normalize(mm(hid, ns[...]))
        new_nodes[at, :] = (nodes[at, :].astype(F32) + out).astype(BF16)
        d_out = norm_back(cot[at, :].astype(F32), out, scale).astype(BF16)
        d_node_out[at, :] = d_out
        d_pre = (mm_nt(d_out, ns[...]) * (sigma * (1.0 + pre * (1.0 - sigma)))).astype(BF16)
        d_node_pre[at, :] = d_pre
        d_tab[at, :] = mm_nt(d_pre, nf[width:, :]).astype(BF16)

    seam_start(2, mm(pick[...], d_tab[0:verts, :]))
    acc[0:width, :] = mm_tn(node_hidden[...], d_node_out[...])
    acc[width : 2 * width, :] = mm_tn(nodes[...], d_node_pre[...])
    acc[2 * width : 3 * width, :] = mm_tn(aggregate[...], d_node_pre[...])
    node_bucket.start_pair()
    wide[...] = cot[...].astype(F32) + mm_nt(d_node_pre[...], nf[:width, :])
    acc[3 * width : 5 * width, :] = jnp.zeros((2 * width, width), F32)
    d_tab[verts : verts + seam, :] = seam_wait(2)
    node_bucket.start_scatter()

    d_edge_pre = msg

    @pl.loop(0, slots // tile)
    def _(i):
        start = pl.multiple_of(i * tile, tile)
        at = pl.ds(start, tile)
        both = (
            jnp.concatenate(
                [ends_hot(cols[0, at, :], verts), jnp.zeros((tile, table - verts), F32)], axis=1
            )
            + ends_hot(cols[1, at, :], table)
        ).astype(BF16)
        d_new = alive_of(start) * mm(both, d_tab[...])
        d_out = norm_back(d_new, normed[at, :], inv[at, :]).astype(BF16)
        d_pre = (mm_nt(d_out, es[...]) * slope[at, :]).astype(BF16)
        d_edge_pre[at, :] = d_pre
        g_edges[at, :] = (d_new + mm_nt(d_pre, ef[:width, :])).astype(BF16)
        acc[3 * width : 4 * width, :] += mm_tn(hidden[at, :], d_out)
        acc[4 * width : 5 * width, :] += mm_tn(edges[at, :], d_pre)

    mid_bucket.start_pair()
    seam_sums = mm(seam_hot, d_edge_pre[...])[:seam].astype(BF16)
    seam_start(3, seam_sums)
    node_bucket.start_gather()

    @pl.loop(0, verts // LANES)
    def _(i):
        start = pl.multiple_of(i * LANES, LANES)
        at = pl.ds(start, LANES)
        sums1[at, :] = mm(hot_rows(0, start).astype(BF16), d_edge_pre[...]).astype(BF16)
        sums2[at, :] = mm(hot_rows(1, start).astype(BF16), d_edge_pre[...])

    mid_bucket.start_scatter()
    acc[5 * width : 6 * width, :] = mm_tn(nodes[...], sums1[...])
    acc[6 * width : 7 * width, :] = mm_tn(nodes[...], sums2[...].astype(BF16)) + mm_tn(
        halo, seam_sums
    )
    end_bucket.start_pair()
    part = wide[...] + mm_nt(sums1[...], ef[width : 2 * width, :])
    end_bucket.start_scatter()
    returned = seam_wait(3)
    second = (sums2[...] + mm_tn(pick[...], returned)).astype(BF16)
    g_nodes[...] = (part + mm_nt(second, ef[2 * width :, :])).astype(BF16)
    mid_bucket.start_gather()
    node_bucket.start_share()
    end_bucket.start_gather()
    mid_bucket.start_share()
    if fused:
        node_bucket.finish([(g_ns, 0, width), (g_nf, 0, 2 * width)])
    end_bucket.start_share()
    if fused:
        mid_bucket.finish([(g_es, 0, width), (g_ef, 0, width)])
        end_bucket.finish([(g_ef, width, 2 * width)])


def write_out(*refs):
    sems = refs[-1]
    half = len(refs) // 2
    copies = [
        pltpu.make_async_copy(refs[i], refs[half + i], sems.at[i]) for i in range(half)
    ]
    for copy in copies:
        copy.start()
    for copy in copies:
        copy.wait()


def local(sizes, nodes, edges, edge_ends, edge_count, send_rows, cotangent, ef, es, nf, ns):
    fused, patches, reps, group = sizes
    verts, width = nodes.shape[1:]
    slots = edges.shape[1]
    hops, slot = send_rows.shape
    seam = hops * slot
    table = verts + -(-seam // LANES) * LANES
    rows = ef.shape[0] + es.shape[0] + nf.shape[0] + ns.shape[0]
    vmem = pl.BlockSpec(memory_space=pltpu.VMEM)
    smem = pl.BlockSpec(memory_space=pltpu.SMEM)
    hbm = pl.BlockSpec(memory_space=pltpu.HBM)

    def like(shape, kind=BF16):
        return jax.ShapeDtypeStruct(shape, kind)

    outs = [like((verts, width)), like((verts, width)), like((slots, width))]
    if fused:
        outs += [like(ef.shape), like(es.shape), like(nf.shape), like(ns.shape)]
    else:
        outs += [like((rows, width), F32)]
    scratch = [pltpu.VMEM((rows, width), F32)] if fused else []
    scratch += [
        pltpu.VMEM((2, slots, LANES), jnp.int32),
        pltpu.VMEM((seam, verts), BF16),
        pltpu.VMEM((verts, width), BF16),
        pltpu.VMEM((table, width), BF16),
        pltpu.VMEM((slots, width), F32),
        pltpu.VMEM((slots, width), F32),
        pltpu.VMEM((slots, 1), F32),
        pltpu.VMEM((slots, width), BF16),
        pltpu.VMEM((slots, width), BF16),
        pltpu.VMEM((4, hops, slot, width), BF16),
        pltpu.VMEM((4, hops, slot, width), BF16),
        pltpu.VMEM((verts, width), F32),
        pltpu.VMEM((verts, width), F32),
        pltpu.VMEM((verts, width), BF16),
        pltpu.VMEM((verts, width), BF16),
        pltpu.VMEM((verts, width), BF16),
        pltpu.VMEM((table, width), BF16),
        pltpu.VMEM((verts, width), BF16),
        pltpu.VMEM((verts, width), F32),
        pltpu.SemaphoreType.DMA((4, hops)),
        pltpu.SemaphoreType.DMA((4, hops)),
    ]
    held = (nodes[0], edges[0], edge_ends.T, send_rows, cotangent[0], ef, es, nf, ns)
    held = tuple(pltpu.with_memory_space_constraint(x, pltpu.HBM) for x in held)
    scratch += [pltpu.VMEM(x.shape, x.dtype) for x in held]
    scratch += [pltpu.SemaphoreType.DMA((len(held),))]
    if fused:
        scratch += [pltpu.VMEM((rows // PACK, PACK, LANES), BF16)] * 6
        scratch += [pltpu.SemaphoreType.DMA((3, 4, group))] * 2
    got = pl.pallas_call(
        functools.partial(body, sizes),
        out_shape=outs,
        in_specs=[hbm] * 3 + [smem] + [hbm] * 6,
        out_specs=[vmem] * len(outs),
        scratch_shapes=scratch,
        compiler_params=pltpu.CompilerParams(
            collective_id=0, has_side_effects=True, vmem_limit_bytes=48 * 2**20
        ),
        name="message_layer",
    )(*held[:3], edge_count, *held[3:])
    got = pl.pallas_call(
        write_out,
        out_shape=outs,
        in_specs=[vmem] * len(outs),
        out_specs=[hbm] * len(outs),
        scratch_shapes=[pltpu.SemaphoreType.DMA((len(outs),))],
        compiler_params=pltpu.CompilerParams(vmem_limit_bytes=2**20),
        name="write_out",
    )(*got)
    new_nodes, g_nodes, g_edges = got[:3]
    if fused:
        g_ef, g_es, g_nf, g_ns = got[3:]
    else:
        total = lax.psum(got[3], ("patch", "rep")).astype(BF16)
        g_ns = total[:width]
        g_nf = total[width : 3 * width]
        g_es = total[3 * width : 4 * width]
        g_ef = total[4 * width :]
    return new_nodes[None], g_nodes[None], g_edges[None], g_ef, g_es, g_nf, g_ns


def solution(mesh):
    patches, reps = mesh.shape["patch"], mesh.shape["rep"]
    group = patches * reps // 2
    fused = reps % 2 == 0 and (2 * LANES) % (PACK * group) == 0
    sizes = (fused, patches, reps, group)
    rows = P("rep", "patch", None)
    placed = (rows, rows, P("patch", None), P("patch"), P("patch", None), rows, P(), P(), P(), P())
    return jax.shard_map(
        functools.partial(local, sizes),
        mesh=mesh,
        in_specs=placed,
        out_specs=(rows, rows, rows, P(), P(), P(), P()),
        check_vma=False,
    )
```

```python
import functools

import jax
import jax.numpy as jnp
from jax import lax
from jax.experimental import pallas as pl
from jax.experimental.pallas import tpu as pltpu
from jax.sharding import PartitionSpec as P

EPS = 1e-05
MESH = pl.DeviceIdType.MESH
F32 = jnp.float32
BF16 = jnp.bfloat16
LANES = 128
PACK = 16


def mm(left, right):
    return jnp.dot(left, right, preferred_element_type=F32)


def mm_nt(left, right):
    return lax.dot_general(left, right, (((1,), (1,)), ((), ())), preferred_element_type=F32)


def mm_tn(left, right):
    return lax.dot_general(left, right, (((0,), (0,)), ((), ())), preferred_element_type=F32)


def normalize(values):
    average = jnp.mean(values, axis=-1, keepdims=True)
    centred = values - average
    inv_scale = lax.rsqrt(jnp.mean(centred * centred, axis=-1, keepdims=True) + EPS)
    return centred * inv_scale, inv_scale


def norm_back(upstream, normed, inv_scale):
    return inv_scale * (
        upstream
        - jnp.mean(upstream, axis=-1, keepdims=True)
        - normed * jnp.mean(upstream * normed, axis=-1, keepdims=True)
    )


def ones_where(mask):
    return jnp.where(mask, 1.0, 0.0).astype(F32)


def as_column(row):
    n = row.shape[1]
    eye = lax.broadcasted_iota(jnp.int32, (n, n), 0) == lax.broadcasted_iota(jnp.int32, (n, n), 1)
    wide = jnp.broadcast_to(row.astype(F32), (n, n))
    return jnp.sum(jnp.where(eye, wide, 0.0), axis=1, keepdims=True)


def tile_of(total, wanted):
    while total % wanted:
        wanted //= 2
    return wanted


def body(sizes, *refs):
    fused, patches, reps, group = sizes
    count = refs[3]
    held = refs[:3] + refs[4:10]
    new_nodes, g_nodes, g_edges = refs[10:13]
    rest = refs[13:]
    if fused:
        g_ef, g_es, g_nf, g_ns, acc = rest[:5]
        rest = rest[5:]
    else:
        acc = rest[0]
        rest = rest[1:]
    (cols, pick, tab1, tab2, slope, normed, inv, hidden, msg, halo_src, halo_dst,
     wide, node_pre, node_hidden, d_node_out, d_node_pre, d_tab, sums1, sums2,
     seam_send, seam_recv) = rest[:21]
    d_new_edge = rest[21]
    (nodes, edges, ends_t, send, cot, ef, es, nf, ns) = rest[22:31]
    loads = rest[31]
    rest = rest[32:]
    if fused:
        pair_out, pair_in, chip_sum, ring_in, final, final_other, ar_send, ar_recv = rest

    verts, width = nodes.shape
    slots = edges.shape[0]
    hops, slot = send.shape
    seam = hops * slot
    table = tab2.shape[0]
    tile = tile_of(slots, 256)
    vtile = tile_of(verts, 256)
    me_p = lax.axis_index("patch")
    me_r = lax.axis_index("rep")

    loaded = [
        pltpu.make_async_copy(src, dst, loads.at[i])
        for i, (src, dst) in enumerate(
            zip(held, (nodes, edges, ends_t, send, cot, ef, es, nf, ns), strict=True)
        )
    ]
    for i in (3, 0, 2, 5, 1, 6, 7, 8, 4):
        loaded[i].start()

    barrier = pltpu.get_barrier_semaphore()
    if fused:
        chips_r = reps // 2
        core = lax.rem(me_r, 2)
        partner = me_r + 1 - 2 * core
        me_g = me_p * chips_r + me_r // 2

        def group_device(k):
            peer = lax.rem(me_g + k, group)
            return peer, {"patch": peer // chips_r, "rep": lax.rem(peer, chips_r) * 2 + core}

        @pl.loop(1, group)
        def _(k):
            _, dev = group_device(k)
            pl.semaphore_signal(barrier, inc=1, device_id=dev, device_id_type=MESH)

        pl.semaphore_signal(barrier, inc=1, device_id={"rep": partner}, device_id_type=MESH)
        greeted = group
    else:
        for step in range(1, hops + 1):
            for other in (lax.rem(me_p + step, patches), lax.rem(me_p + patches - step, patches)):
                pl.semaphore_signal(
                    barrier, inc=1, device_id={"patch": other}, device_id_type=MESH
                )
        greeted = 2 * hops

    def seam_copies(stage):
        down = stage % 2 == 0
        made = []
        for h in range(hops):
            step = patches - h - 1 if down else h + 1
            made.append(
                pltpu.make_async_remote_copy(
                    src_ref=halo_src.at[stage, h],
                    dst_ref=halo_dst.at[stage, h],
                    send_sem=seam_send.at[stage, h],
                    recv_sem=seam_recv.at[stage, h],
                    device_id={"patch": lax.rem(me_p + step, patches)},
                    device_id_type=MESH,
                )
            )
        return made

    def seam_start(stage, values):
        if values is not None:
            for h in range(hops):
                halo_src[stage, h] = values[h * slot : (h + 1) * slot].astype(BF16)
        for copy in seam_copies(stage):
            copy.start()

    def seam_wait(stage):
        for copy in seam_copies(stage):
            copy.wait()
        return jnp.concatenate([halo_dst[stage, h] for h in range(hops)], axis=0)

    class Bucket:
        def __init__(self, index, row, rows):
            self.index, self.row, self.rows = index, row, rows
            self.first = row // PACK
            self.blocks = rows // PACK
            if fused:
                self.own = self.blocks // group

        def pair(self, phase, src, dst):
            span = pl.ds(self.first, self.blocks)
            return pltpu.make_async_remote_copy(
                src_ref=src.at[span],
                dst_ref=dst.at[span],
                send_sem=ar_send.at[self.index, phase, 0],
                recv_sem=ar_recv.at[self.index, phase, 0],
                device_id={"rep": partner},
                device_id_type=MESH,
            )

        def scatter_copy(self, k):
            peer, dev = group_device(k)
            return pltpu.make_async_remote_copy(
                src_ref=chip_sum.at[pl.ds(self.first + peer * self.own, self.own)],
                dst_ref=ring_in.at[pl.ds(self.first + k * self.own, self.own)],
                send_sem=ar_send.at[self.index, 1, k],
                recv_sem=ar_recv.at[self.index, 1, k],
                device_id=dev,
                device_id_type=MESH,
            )

        def gather_copy(self, k):
            _, dev = group_device(k)
            mine = pl.ds(self.first + me_g * self.own, self.own)
            return pltpu.make_async_remote_copy(
                src_ref=final.at[mine],
                dst_ref=final.at[mine],
                send_sem=ar_send.at[self.index, 2, k],
                recv_sem=ar_recv.at[self.index, 2, k],
                device_id=dev,
                device_id_type=MESH,
            )

        def halves(self):
            low = acc[self.row : self.row + self.rows, :LANES]
            high = acc[self.row : self.row + self.rows, LANES:]
            return low, high

        def start_pair(self):
            if not fused:
                return
            low, high = self.halves()
            other = jnp.where(core == 0, high, low)
            pair_out[self.first : self.first + self.blocks] = other.astype(BF16).reshape(
                self.blocks, PACK, LANES
            )
            self.pair(0, pair_out, pair_in).start()

        def start_scatter(self):
            if not fused:
                return
            self.pair(0, pair_out, pair_in).wait()
            low, high = self.halves()
            mine = jnp.where(core == 0, low, high).reshape(self.blocks, PACK, LANES)
            got = pair_in[self.first : self.first + self.blocks].astype(F32)
            chip_sum[self.first : self.first + self.blocks] = (mine + got).astype(BF16)

            @pl.loop(1, group)
            def _(k):
                self.scatter_copy(k).start()

        def start_gather(self):
            if not fused:
                return

            @pl.loop(1, group)
            def _(k):
                self.scatter_copy(k).wait()

            mine = pl.ds(self.first + me_g * self.own, self.own)
            total = chip_sum[mine].astype(F32)
            for k in range(1, group):
                at = self.first + k * self.own
                total = total + ring_in[at : at + self.own].astype(F32)
            final[mine] = total.astype(BF16)

            @pl.loop(1, group)
            def _(k):
                self.gather_copy(k).start()

        def start_share(self):
            if not fused:
                return

            @pl.loop(1, group)
            def _(k):
                self.gather_copy(k).wait()

            self.pair(3, final, final_other).start()

        def finish(self, targets):
            if not fused:
                return
            self.pair(3, final, final_other).wait()
            at = self.first
            for ref, row, rows in targets:
                n = rows // PACK
                a = final[at : at + n].reshape(rows, LANES)
                b = final_other[at : at + n].reshape(rows, LANES)
                ref[row : row + rows, :LANES] = jnp.where(core == 0, a, b)
                ref[row : row + rows, LANES:] = jnp.where(core == 0, b, a)
                at += n

    node_bucket = Bucket(0, 0, 3 * width)
    mid_bucket = Bucket(1, 3 * width, 2 * width)
    end_bucket = Bucket(2, 5 * width, 2 * width)

    loaded[3].wait()
    loaded[0].wait()
    lane_v = lax.broadcasted_iota(jnp.int32, (slot, verts), 1).astype(F32)
    for h in range(hops):
        chosen = as_column(send[h : h + 1, :])
        pick[h * slot : (h + 1) * slot, :] = ones_where(lane_v == chosen).astype(BF16)
    outgoing = mm(pick[...], nodes[...])
    for h in range(hops):
        halo_src[0, h] = outgoing[h * slot : (h + 1) * slot].astype(BF16)

    loaded[2].wait()
    @pl.loop(0, slots // LANES)
    def _(j):
        at = pl.ds(pl.multiple_of(j * LANES, LANES), LANES)
        for end in range(2):
            column = as_column(ends_t[end : end + 1, at])
            cols[end, at, :] = jnp.broadcast_to(column, (LANES, LANES)).astype(jnp.int32)

    loaded[5].wait()
    tab1[...] = mm(nodes[...], ef[width : 2 * width, :]).astype(BF16)
    tab2[0:verts, :] = mm(nodes[...], ef[2 * width :, :]).astype(BF16)
    if table > verts + seam:
        tab2[verts + seam :, :] = jnp.zeros((table - verts - seam, width), BF16)
        d_tab[verts + seam :, :] = jnp.zeros((table - verts - seam, width), BF16)
    lane_e = lax.broadcasted_iota(jnp.int32, (tile, LANES), 1)

    def ends_hot(column, size):
        return jnp.concatenate(
            [ones_where(column == lane_e + k) for k in range(0, size, LANES)], axis=1
        )

    def alive_of(start):
        at = lax.broadcasted_iota(jnp.int32, (tile, 1), 0) + start
        return ones_where(at < count[0])

    def halo_hot(at):
        return jnp.concatenate(
            [ones_where(cols[1, at, :] == lane_e + k) for k in range(verts, table, LANES)], axis=1
        ).astype(BF16)

    def local_pre(i):
        at = pl.ds(pl.multiple_of(i * tile, tile), tile)
        first = ends_hot(cols[0, at, :], verts).astype(BF16)
        second = ends_hot(cols[1, at, :], verts).astype(BF16)
        slope[at, :] = (
            mm(edges[at, :], ef[:width, :]) + mm(first, tab1[...]) + mm(second, tab2[:verts, :])
        )

    loaded[1].wait()
    tiles = slots // tile
    pl.loop(0, tiles // 3)(local_pre)
    pl.semaphore_wait(barrier, greeted)
    seam_start(0, None)
    pl.loop(tiles // 3, tiles)(local_pre)
    loaded[6].wait()
    halo = seam_wait(0)
    tab2[verts : verts + seam, :] = mm(halo, ef[2 * width :, :]).astype(BF16)

    @pl.loop(0, tiles)
    def _(i):
        start = pl.multiple_of(i * tile, tile)
        at = pl.ds(start, tile)
        rows = edges[at, :]
        pre = slope[at, :] + mm(halo_hot(at), tab2[verts:, :])
        sigma = jax.nn.sigmoid(pre)
        hid = (pre * sigma).astype(BF16)
        slope[at, :] = sigma * (1.0 + pre * (1.0 - sigma))
        hidden[at, :] = hid
        out, scale = normalize(mm(hid, es[...]))
        normed[at, :] = out
        inv[at, :] = scale
        msg[at, :] = (alive_of(start) * (rows.astype(F32) + out)).astype(BF16)

    sub_v = lax.broadcasted_iota(jnp.int32, (LANES, slots), 0)

    def hot_rows(end, start):
        return ones_where(ends_t[end : end + 1, :] == sub_v + start)

    seam_hot = hot_rows(1, verts).astype(BF16)
    seam_start(1, mm(seam_hot, msg[...])[:seam])

    @pl.loop(0, verts // LANES)
    def _(i):
        start = pl.multiple_of(i * LANES, LANES)
        both = (hot_rows(0, start) + hot_rows(1, start)).astype(BF16)
        wide[pl.ds(start, LANES), :] = mm(both, msg[...])

    for i in (7, 8, 4):
        loaded[i].wait()
    node_pre[...] = mm(nodes[...], nf[:width, :])
    returned = seam_wait(1)
    wide[...] += mm_tn(pick[...], returned)
    aggregate = tab1
    aggregate[...] = wide[...].astype(BF16)

    @pl.loop(0, verts // vtile)
    def _(i):
        at = pl.ds(pl.multiple_of(i * vtile, vtile), vtile)
        pre = node_pre[at, :] + mm(aggregate[at, :], nf[width:, :])
        sigma = jax.nn.sigmoid(pre)
        hid = (pre * sigma).astype(BF16)
        node_hidden[at, :] = hid
        out, scale = normalize(mm(hid, ns[...]))
        new_nodes[at, :] = (nodes[at, :].astype(F32) + out).astype(BF16)
        d_out = norm_back(cot[at, :].astype(F32), out, scale).astype(BF16)
        d_node_out[at, :] = d_out
        d_pre = (mm_nt(d_out, ns[...]) * (sigma * (1.0 + pre * (1.0 - sigma)))).astype(BF16)
        d_node_pre[at, :] = d_pre
        d_tab[at, :] = mm_nt(d_pre, nf[width:, :]).astype(BF16)

    seam_start(2, mm(pick[...], d_tab[0:verts, :]))
    acc[0:width, :] = mm_tn(node_hidden[...], d_node_out[...])
    acc[width : 2 * width, :] = mm_tn(nodes[...], d_node_pre[...])
    acc[2 * width : 3 * width, :] = mm_tn(aggregate[...], d_node_pre[...])
    node_bucket.start_pair()
    wide[...] = cot[...].astype(F32) + mm_nt(d_node_pre[...], nf[:width, :])
    acc[3 * width : 5 * width, :] = jnp.zeros((2 * width, width), F32)

    def local_d_new(i):
        at = pl.ds(pl.multiple_of(i * tile, tile), tile)
        both = (ends_hot(cols[0, at, :], verts) + ends_hot(cols[1, at, :], verts)).astype(BF16)
        d_new_edge[at, :] = mm(both, d_tab[:verts, :])

    pl.loop(0, tiles // 2)(local_d_new)
    node_bucket.start_scatter()
    pl.loop(tiles // 2, tiles)(local_d_new)
    d_tab[verts : verts + seam, :] = seam_wait(2)

    d_edge_pre = msg

    @pl.loop(0, tiles)
    def _(i):
        start = pl.multiple_of(i * tile, tile)
        at = pl.ds(start, tile)
        d_new = alive_of(start) * (d_new_edge[at, :] + mm(halo_hot(at), d_tab[verts:, :]))
        d_new_edge[at, :] = d_new
        d_out = norm_back(d_new, normed[at, :], inv[at, :]).astype(BF16)
        d_pre = (mm_nt(d_out, es[...]) * slope[at, :]).astype(BF16)
        d_edge_pre[at, :] = d_pre
        acc[3 * width : 4 * width, :] += mm_tn(hidden[at, :], d_out)
        acc[4 * width : 5 * width, :] += mm_tn(edges[at, :], d_pre)

    mid_bucket.start_pair()
    seam_sums = mm(seam_hot, d_edge_pre[...])[:seam].astype(BF16)
    seam_start(3, seam_sums)
    node_bucket.start_gather()

    @pl.loop(0, verts // LANES)
    def _(i):
        start = pl.multiple_of(i * LANES, LANES)
        at = pl.ds(start, LANES)
        sums1[at, :] = mm(hot_rows(0, start).astype(BF16), d_edge_pre[...]).astype(BF16)
        sums2[at, :] = mm(hot_rows(1, start).astype(BF16), d_edge_pre[...])

    mid_bucket.start_scatter()
    acc[5 * width : 6 * width, :] = mm_tn(nodes[...], sums1[...])
    acc[6 * width : 7 * width, :] = mm_tn(nodes[...], sums2[...].astype(BF16)) + mm_tn(
        halo, seam_sums
    )
    end_bucket.start_pair()
    part = wide[...] + mm_nt(sums1[...], ef[width : 2 * width, :])
    end_bucket.start_scatter()

    @pl.loop(0, tiles)
    def _(i):
        at = pl.ds(pl.multiple_of(i * tile, tile), tile)
        g_edges[at, :] = (d_new_edge[at, :] + mm_nt(d_edge_pre[at, :], ef[:width, :])).astype(BF16)

    returned = seam_wait(3)
    second = (sums2[...] + mm_tn(pick[...], returned)).astype(BF16)
    g_nodes[...] = (part + mm_nt(second, ef[2 * width :, :])).astype(BF16)
    mid_bucket.start_gather()
    node_bucket.start_share()
    end_bucket.start_gather()
    mid_bucket.start_share()
    if fused:
        node_bucket.finish([(g_ns, 0, width), (g_nf, 0, 2 * width)])
    end_bucket.start_share()
    if fused:
        mid_bucket.finish([(g_es, 0, width), (g_ef, 0, width)])
        end_bucket.finish([(g_ef, width, 2 * width)])


def write_out(*refs):
    sems = refs[-1]
    half = len(refs) // 2
    copies = [
        pltpu.make_async_copy(refs[i], refs[half + i], sems.at[i]) for i in range(half)
    ]
    for copy in copies:
        copy.start()
    for copy in copies:
        copy.wait()


def local(sizes, nodes, edges, edge_ends, edge_count, send_rows, cotangent, ef, es, nf, ns):
    fused, patches, reps, group = sizes
    verts, width = nodes.shape[1:]
    slots = edges.shape[1]
    hops, slot = send_rows.shape
    seam = hops * slot
    table = verts + -(-seam // LANES) * LANES
    rows = ef.shape[0] + es.shape[0] + nf.shape[0] + ns.shape[0]
    vmem = pl.BlockSpec(memory_space=pltpu.VMEM)
    smem = pl.BlockSpec(memory_space=pltpu.SMEM)
    hbm = pl.BlockSpec(memory_space=pltpu.HBM)

    def like(shape, kind=BF16):
        return jax.ShapeDtypeStruct(shape, kind)

    outs = [like((verts, width)), like((verts, width)), like((slots, width))]
    if fused:
        outs += [like(ef.shape), like(es.shape), like(nf.shape), like(ns.shape)]
    else:
        outs += [like((rows, width), F32)]
    scratch = [pltpu.VMEM((rows, width), F32)] if fused else []
    scratch += [
        pltpu.VMEM((2, slots, LANES), jnp.int32),
        pltpu.VMEM((seam, verts), BF16),
        pltpu.VMEM((verts, width), BF16),
        pltpu.VMEM((table, width), BF16),
        pltpu.VMEM((slots, width), F32),
        pltpu.VMEM((slots, width), F32),
        pltpu.VMEM((slots, 1), F32),
        pltpu.VMEM((slots, width), BF16),
        pltpu.VMEM((slots, width), BF16),
        pltpu.VMEM((4, hops, slot, width), BF16),
        pltpu.VMEM((4, hops, slot, width), BF16),
        pltpu.VMEM((verts, width), F32),
        pltpu.VMEM((verts, width), F32),
        pltpu.VMEM((verts, width), BF16),
        pltpu.VMEM((verts, width), BF16),
        pltpu.VMEM((verts, width), BF16),
        pltpu.VMEM((table, width), BF16),
        pltpu.VMEM((verts, width), BF16),
        pltpu.VMEM((verts, width), F32),
        pltpu.SemaphoreType.DMA((4, hops)),
        pltpu.SemaphoreType.DMA((4, hops)),
        pltpu.VMEM((slots, width), F32),
    ]
    held = (nodes[0], edges[0], edge_ends.T, send_rows, cotangent[0], ef, es, nf, ns)
    held = tuple(pltpu.with_memory_space_constraint(x, pltpu.HBM) for x in held)
    scratch += [pltpu.VMEM(x.shape, x.dtype) for x in held]
    scratch += [pltpu.SemaphoreType.DMA((len(held),))]
    if fused:
        scratch += [pltpu.VMEM((rows // PACK, PACK, LANES), BF16)] * 6
        scratch += [pltpu.SemaphoreType.DMA((3, 4, group))] * 2
    got = pl.pallas_call(
        functools.partial(body, sizes),
        out_shape=outs,
        in_specs=[hbm] * 3 + [smem] + [hbm] * 6,
        out_specs=[vmem] * len(outs),
        scratch_shapes=scratch,
        compiler_params=pltpu.CompilerParams(
            collective_id=0, has_side_effects=True, vmem_limit_bytes=48 * 2**20
        ),
        name="message_layer",
    )(*held[:3], edge_count, *held[3:])
    got = pl.pallas_call(
        write_out,
        out_shape=outs,
        in_specs=[vmem] * len(outs),
        out_specs=[hbm] * len(outs),
        scratch_shapes=[pltpu.SemaphoreType.DMA((len(outs),))],
        compiler_params=pltpu.CompilerParams(vmem_limit_bytes=2**20),
        name="write_out",
    )(*got)
    new_nodes, g_nodes, g_edges = got[:3]
    if fused:
        g_ef, g_es, g_nf, g_ns = got[3:]
    else:
        total = lax.psum(got[3], ("patch", "rep")).astype(BF16)
        g_ns = total[:width]
        g_nf = total[width : 3 * width]
        g_es = total[3 * width : 4 * width]
        g_ef = total[4 * width :]
    return new_nodes[None], g_nodes[None], g_edges[None], g_ef, g_es, g_nf, g_ns


def solution(mesh):
    patches, reps = mesh.shape["patch"], mesh.shape["rep"]
    group = patches * reps // 2
    fused = reps % 2 == 0 and (2 * LANES) % (PACK * group) == 0
    sizes = (fused, patches, reps, group)
    rows = P("rep", "patch", None)
    placed = (rows, rows, P("patch", None), P("patch"), P("patch", None), rows, P(), P(), P(), P())
    return jax.shard_map(
        functools.partial(local, sizes),
        mesh=mesh,
        in_specs=placed,
        out_specs=(rows, rows, rows, P(), P(), P(), P()),
        check_vma=False,
    )
```

```python
import functools

import jax
import jax.numpy as jnp
from jax import lax
from jax.experimental import pallas as pl
from jax.experimental.pallas import tpu as pltpu
from jax.sharding import PartitionSpec as P

EPS = 1e-05
MESH = pl.DeviceIdType.MESH
F32 = jnp.float32
BF16 = jnp.bfloat16
LANES = 128
PACK = 16
INNER = 2


def mm(left, right):
    return jnp.dot(left, right, preferred_element_type=F32)


def mm_nt(left, right):
    return lax.dot_general(left, right, (((1,), (1,)), ((), ())), preferred_element_type=F32)


def mm_tn(left, right):
    return lax.dot_general(left, right, (((0,), (0,)), ((), ())), preferred_element_type=F32)


def normalize(values):
    average = jnp.mean(values, axis=-1, keepdims=True)
    centred = values - average
    inv_scale = lax.rsqrt(jnp.mean(centred * centred, axis=-1, keepdims=True) + EPS)
    return centred * inv_scale, inv_scale


def norm_back(upstream, normed, inv_scale):
    return inv_scale * (
        upstream
        - jnp.mean(upstream, axis=-1, keepdims=True)
        - normed * jnp.mean(upstream * normed, axis=-1, keepdims=True)
    )


def ones_where(mask):
    return jnp.where(mask, 1.0, 0.0).astype(F32)


def as_column(row):
    n = row.shape[1]
    eye = lax.broadcasted_iota(jnp.int32, (n, n), 0) == lax.broadcasted_iota(jnp.int32, (n, n), 1)
    wide = jnp.broadcast_to(row.astype(F32), (n, n))
    return jnp.sum(jnp.where(eye, wide, 0.0), axis=1, keepdims=True)


def tile_of(total, wanted):
    while total % wanted:
        wanted //= 2
    return wanted


def body(sizes, *refs):
    fused, patches, reps, group = sizes
    count = refs[3]
    held = refs[:3] + refs[4:10]
    new_nodes, g_nodes, g_edges = refs[10:13]
    rest = refs[13:]
    if fused:
        g_ef, g_es, g_nf, g_ns, acc = rest[:5]
        rest = rest[5:]
    else:
        acc = rest[0]
        rest = rest[1:]
    (cols, pick, tab1, tab2, slope, normed, inv, hidden, msg, halo_src, halo_dst,
     wide, node_pre, node_hidden, d_node_out, d_node_pre, d_tab, sums1, sums2,
     seam_send, seam_recv) = rest[:21]
    d_new_edge = rest[21]
    (nodes, edges, ends_t, send, cot, ef, es, nf, ns) = rest[22:31]
    loads = rest[31]
    rest = rest[32:]
    if fused:
        pair_out, pair_in, chip_sum, ring_in, final, final_other, line_sum, ar_send, ar_recv = rest

    verts, width = nodes.shape
    slots = edges.shape[0]
    hops, slot = send.shape
    seam = hops * slot
    table = tab2.shape[0]
    tile = tile_of(slots, 256)
    vtile = tile_of(verts, 256)
    me_p = lax.axis_index("patch")
    me_r = lax.axis_index("rep")

    loaded = [
        pltpu.make_async_copy(src, dst, loads.at[i])
        for i, (src, dst) in enumerate(
            zip(held, (nodes, edges, ends_t, send, cot, ef, es, nf, ns), strict=True)
        )
    ]
    for i in (3, 0, 2, 5, 1, 6, 7, 8, 4):
        loaded[i].start()

    barrier = pltpu.get_barrier_semaphore()
    if fused:
        chips_r = reps // 2
        core = lax.rem(me_r, 2)
        partner = me_r + 1 - 2 * core
        quad, lines = INNER * chips_r, patches // INNER
        me_l, me_y = me_p // INNER, lax.rem(me_p, INNER)
        me_q = me_y * chips_r + me_r // 2

        def quad_device(k):
            peer = lax.rem(me_q + k, quad)
            return peer, {
                "patch": me_l * INNER + peer // chips_r,
                "rep": lax.rem(peer, chips_r) * 2 + core,
            }

        def line_device(k):
            return {"patch": lax.rem(me_l + k, lines) * INNER + me_y}

        def greet(device):
            pl.semaphore_signal(barrier, inc=1, device_id=device, device_id_type=MESH)

        for k in range(1, quad):
            greet(quad_device(k)[1])
        for k in range(1, lines):
            greet(line_device(k))
        greet({"rep": partner})
        greeted = quad + lines - 1
    else:
        greeted = 0
    for step in range(1, hops + 1):
        for other in (lax.rem(me_p + step, patches), lax.rem(me_p + patches - step, patches)):
            pl.semaphore_signal(barrier, inc=1, device_id={"patch": other}, device_id_type=MESH)
    greeted += 2 * hops

    def seam_copies(stage):
        down = stage % 2 == 0
        made = []
        for h in range(hops):
            step = patches - h - 1 if down else h + 1
            made.append(
                pltpu.make_async_remote_copy(
                    src_ref=halo_src.at[stage, h],
                    dst_ref=halo_dst.at[stage, h],
                    send_sem=seam_send.at[stage, h],
                    recv_sem=seam_recv.at[stage, h],
                    device_id={"patch": lax.rem(me_p + step, patches)},
                    device_id_type=MESH,
                )
            )
        return made

    def seam_start(stage, values):
        if values is not None:
            for h in range(hops):
                halo_src[stage, h] = values[h * slot : (h + 1) * slot].astype(BF16)
        for copy in seam_copies(stage):
            copy.start()

    def seam_wait(stage):
        for copy in seam_copies(stage):
            copy.wait()
        return jnp.concatenate([halo_dst[stage, h] for h in range(hops)], axis=0)

    class Bucket:
        def __init__(self, index, row, rows):
            self.index, self.row, self.rows = index, row, rows
            self.first = row // PACK
            self.blocks = rows // PACK
            if fused:
                self.own = self.blocks // quad
                self.line_first = self.first * lines // quad

        def pair(self, phase, src, dst):
            span = pl.ds(self.first, self.blocks)
            return pltpu.make_async_remote_copy(
                src_ref=src.at[span],
                dst_ref=dst.at[span],
                send_sem=ar_send.at[self.index, phase, 0],
                recv_sem=ar_recv.at[self.index, phase, 0],
                device_id={"rep": partner},
                device_id_type=MESH,
            )

        def scatter_copy(self, k):
            peer, dev = quad_device(k)
            return pltpu.make_async_remote_copy(
                src_ref=chip_sum.at[pl.ds(self.first + peer * self.own, self.own)],
                dst_ref=ring_in.at[pl.ds(self.first + k * self.own, self.own)],
                send_sem=ar_send.at[self.index, 1, k],
                recv_sem=ar_recv.at[self.index, 1, k],
                device_id=dev,
                device_id_type=MESH,
            )

        def line_copy(self, k):
            mine = pl.ds(self.line_first + me_l * self.own, self.own)
            return pltpu.make_async_remote_copy(
                src_ref=line_sum.at[mine],
                dst_ref=line_sum.at[mine],
                send_sem=ar_send.at[self.index, 2, k],
                recv_sem=ar_recv.at[self.index, 2, k],
                device_id=line_device(k),
                device_id_type=MESH,
            )

        def gather_copy(self, k):
            _, dev = quad_device(k)
            mine = pl.ds(self.first + me_q * self.own, self.own)
            return pltpu.make_async_remote_copy(
                src_ref=final.at[mine],
                dst_ref=final.at[mine],
                send_sem=ar_send.at[self.index, 3, k],
                recv_sem=ar_recv.at[self.index, 3, k],
                device_id=dev,
                device_id_type=MESH,
            )

        def halves(self):
            low = acc[self.row : self.row + self.rows, :LANES]
            high = acc[self.row : self.row + self.rows, LANES:]
            return low, high

        def start_pair(self):
            if not fused:
                return
            low, high = self.halves()
            other = jnp.where(core == 0, high, low)
            pair_out[self.first : self.first + self.blocks] = other.astype(BF16).reshape(
                self.blocks, PACK, LANES
            )
            self.pair(0, pair_out, pair_in).start()

        def start_scatter(self):
            if not fused:
                return
            self.pair(0, pair_out, pair_in).wait()
            low, high = self.halves()
            mine = jnp.where(core == 0, low, high).reshape(self.blocks, PACK, LANES)
            got = pair_in[self.first : self.first + self.blocks].astype(F32)
            chip_sum[self.first : self.first + self.blocks] = (mine + got).astype(BF16)

            for k in range(1, quad):
                self.scatter_copy(k).start()

        def start_line(self):
            if not fused:
                return
            total = chip_sum[pl.ds(self.first + me_q * self.own, self.own)].astype(F32)
            for k in range(1, quad):
                self.scatter_copy(k).wait()
                at = self.first + k * self.own
                total = total + ring_in[at : at + self.own].astype(F32)
            line_sum[pl.ds(self.line_first + me_l * self.own, self.own)] = total.astype(BF16)
            for k in range(1, lines):
                self.line_copy(k).start()

        def start_gather(self):
            if not fused:
                return
            for k in range(1, lines):
                self.line_copy(k).wait()
            total = line_sum[self.line_first : self.line_first + self.own].astype(F32)
            for k in range(1, lines):
                at = self.line_first + k * self.own
                total = total + line_sum[at : at + self.own].astype(F32)
            final[pl.ds(self.first + me_q * self.own, self.own)] = total.astype(BF16)
            for k in range(1, quad):
                self.gather_copy(k).start()

        def start_share(self):
            if not fused:
                return
            for k in range(1, quad):
                self.gather_copy(k).wait()
            self.pair(4, final, final_other).start()

        def finish(self, targets):
            if not fused:
                return
            self.pair(4, final, final_other).wait()
            at = self.first
            for ref, row, rows in targets:
                n = rows // PACK
                a = final[at : at + n].reshape(rows, LANES)
                b = final_other[at : at + n].reshape(rows, LANES)
                ref[row : row + rows, :LANES] = jnp.where(core == 0, a, b)
                ref[row : row + rows, LANES:] = jnp.where(core == 0, b, a)
                at += n

    node_bucket = Bucket(0, 0, 3 * width)
    mid_bucket = Bucket(1, 3 * width, 2 * width)
    end_bucket = Bucket(2, 5 * width, 2 * width)

    loaded[3].wait()
    loaded[0].wait()
    lane_v = lax.broadcasted_iota(jnp.int32, (slot, verts), 1).astype(F32)
    for h in range(hops):
        chosen = as_column(send[h : h + 1, :])
        pick[h * slot : (h + 1) * slot, :] = ones_where(lane_v == chosen).astype(BF16)
    outgoing = mm(pick[...], nodes[...])
    for h in range(hops):
        halo_src[0, h] = outgoing[h * slot : (h + 1) * slot].astype(BF16)

    loaded[2].wait()
    @pl.loop(0, slots // LANES)
    def _(j):
        at = pl.ds(pl.multiple_of(j * LANES, LANES), LANES)
        for end in range(2):
            column = as_column(ends_t[end : end + 1, at])
            cols[end, at, :] = jnp.broadcast_to(column, (LANES, LANES)).astype(jnp.int32)

    loaded[5].wait()
    tab1[...] = mm(nodes[...], ef[width : 2 * width, :]).astype(BF16)
    tab2[0:verts, :] = mm(nodes[...], ef[2 * width :, :]).astype(BF16)
    if table > verts + seam:
        tab2[verts + seam :, :] = jnp.zeros((table - verts - seam, width), BF16)
        d_tab[verts + seam :, :] = jnp.zeros((table - verts - seam, width), BF16)
    lane_e = lax.broadcasted_iota(jnp.int32, (tile, LANES), 1)

    def ends_hot(column, size):
        return jnp.concatenate(
            [ones_where(column == lane_e + k) for k in range(0, size, LANES)], axis=1
        )

    def alive_of(start):
        at = lax.broadcasted_iota(jnp.int32, (tile, 1), 0) + start
        return ones_where(at < count[0])

    def halo_hot(at):
        return jnp.concatenate(
            [ones_where(cols[1, at, :] == lane_e + k) for k in range(verts, table, LANES)], axis=1
        ).astype(BF16)

    def local_pre(i):
        at = pl.ds(pl.multiple_of(i * tile, tile), tile)
        first = ends_hot(cols[0, at, :], verts).astype(BF16)
        second = ends_hot(cols[1, at, :], verts).astype(BF16)
        slope[at, :] = (
            mm(edges[at, :], ef[:width, :]) + mm(first, tab1[...]) + mm(second, tab2[:verts, :])
        )

    loaded[1].wait()
    tiles = slots // tile
    pl.loop(0, tiles // 3)(local_pre)
    pl.semaphore_wait(barrier, greeted)
    seam_start(0, None)
    pl.loop(tiles // 3, tiles)(local_pre)
    loaded[6].wait()
    halo = seam_wait(0)
    tab2[verts : verts + seam, :] = mm(halo, ef[2 * width :, :]).astype(BF16)

    @pl.loop(0, tiles)
    def _(i):
        start = pl.multiple_of(i * tile, tile)
        at = pl.ds(start, tile)
        rows = edges[at, :]
        pre = slope[at, :] + mm(halo_hot(at), tab2[verts:, :])
        sigma = jax.nn.sigmoid(pre)
        hid = (pre * sigma).astype(BF16)
        slope[at, :] = sigma * (1.0 + pre * (1.0 - sigma))
        hidden[at, :] = hid
        out, scale = normalize(mm(hid, es[...]))
        normed[at, :] = out
        inv[at, :] = scale
        msg[at, :] = (alive_of(start) * (rows.astype(F32) + out)).astype(BF16)

    sub_v = lax.broadcasted_iota(jnp.int32, (LANES, slots), 0)

    def hot_rows(end, start):
        return ones_where(ends_t[end : end + 1, :] == sub_v + start)

    seam_hot = hot_rows(1, verts).astype(BF16)
    seam_start(1, mm(seam_hot, msg[...])[:seam])

    @pl.loop(0, verts // LANES)
    def _(i):
        start = pl.multiple_of(i * LANES, LANES)
        both = (hot_rows(0, start) + hot_rows(1, start)).astype(BF16)
        wide[pl.ds(start, LANES), :] = mm(both, msg[...])

    for i in (7, 8, 4):
        loaded[i].wait()
    node_pre[...] = mm(nodes[...], nf[:width, :])
    returned = seam_wait(1)
    wide[...] += mm_tn(pick[...], returned)
    aggregate = tab1
    aggregate[...] = wide[...].astype(BF16)

    @pl.loop(0, verts // vtile)
    def _(i):
        at = pl.ds(pl.multiple_of(i * vtile, vtile), vtile)
        pre = node_pre[at, :] + mm(aggregate[at, :], nf[width:, :])
        sigma = jax.nn.sigmoid(pre)
        hid = (pre * sigma).astype(BF16)
        node_hidden[at, :] = hid
        out, scale = normalize(mm(hid, ns[...]))
        new_nodes[at, :] = (nodes[at, :].astype(F32) + out).astype(BF16)
        d_out = norm_back(cot[at, :].astype(F32), out, scale).astype(BF16)
        d_node_out[at, :] = d_out
        d_pre = (mm_nt(d_out, ns[...]) * (sigma * (1.0 + pre * (1.0 - sigma)))).astype(BF16)
        d_node_pre[at, :] = d_pre
        d_tab[at, :] = mm_nt(d_pre, nf[width:, :]).astype(BF16)

    seam_start(2, mm(pick[...], d_tab[0:verts, :]))
    acc[0:width, :] = mm_tn(node_hidden[...], d_node_out[...])
    acc[width : 2 * width, :] = mm_tn(nodes[...], d_node_pre[...])
    acc[2 * width : 3 * width, :] = mm_tn(aggregate[...], d_node_pre[...])
    node_bucket.start_pair()
    wide[...] = cot[...].astype(F32) + mm_nt(d_node_pre[...], nf[:width, :])
    acc[3 * width : 5 * width, :] = jnp.zeros((2 * width, width), F32)

    def local_d_new(i):
        at = pl.ds(pl.multiple_of(i * tile, tile), tile)
        both = (ends_hot(cols[0, at, :], verts) + ends_hot(cols[1, at, :], verts)).astype(BF16)
        d_new_edge[at, :] = mm(both, d_tab[:verts, :])

    pl.loop(0, tiles // 2)(local_d_new)
    node_bucket.start_scatter()
    pl.loop(tiles // 2, tiles)(local_d_new)
    d_tab[verts : verts + seam, :] = seam_wait(2)

    d_edge_pre = msg

    @pl.loop(0, tiles)
    def _(i):
        start = pl.multiple_of(i * tile, tile)
        at = pl.ds(start, tile)
        d_new = alive_of(start) * (d_new_edge[at, :] + mm(halo_hot(at), d_tab[verts:, :]))
        d_new_edge[at, :] = d_new
        d_out = norm_back(d_new, normed[at, :], inv[at, :]).astype(BF16)
        d_pre = (mm_nt(d_out, es[...]) * slope[at, :]).astype(BF16)
        d_edge_pre[at, :] = d_pre
        acc[3 * width : 4 * width, :] += mm_tn(hidden[at, :], d_out)
        acc[4 * width : 5 * width, :] += mm_tn(edges[at, :], d_pre)

    mid_bucket.start_pair()
    seam_sums = mm(seam_hot, d_edge_pre[...])[:seam].astype(BF16)
    seam_start(3, seam_sums)
    node_bucket.start_line()

    @pl.loop(0, verts // LANES)
    def _(i):
        start = pl.multiple_of(i * LANES, LANES)
        at = pl.ds(start, LANES)
        sums1[at, :] = mm(hot_rows(0, start).astype(BF16), d_edge_pre[...]).astype(BF16)
        sums2[at, :] = mm(hot_rows(1, start).astype(BF16), d_edge_pre[...])

    mid_bucket.start_scatter()
    node_bucket.start_gather()
    acc[5 * width : 6 * width, :] = mm_tn(nodes[...], sums1[...])
    acc[6 * width : 7 * width, :] = mm_tn(nodes[...], sums2[...].astype(BF16)) + mm_tn(
        halo, seam_sums
    )
    end_bucket.start_pair()
    part = wide[...] + mm_nt(sums1[...], ef[width : 2 * width, :])
    mid_bucket.start_line()
    end_bucket.start_scatter()

    @pl.loop(0, tiles)
    def _(i):
        at = pl.ds(pl.multiple_of(i * tile, tile), tile)
        g_edges[at, :] = (d_new_edge[at, :] + mm_nt(d_edge_pre[at, :], ef[:width, :])).astype(BF16)

    end_bucket.start_line()
    returned = seam_wait(3)
    second = (sums2[...] + mm_tn(pick[...], returned)).astype(BF16)
    g_nodes[...] = (part + mm_nt(second, ef[2 * width :, :])).astype(BF16)
    mid_bucket.start_gather()
    node_bucket.start_share()
    end_bucket.start_gather()
    mid_bucket.start_share()
    if fused:
        node_bucket.finish([(g_ns, 0, width), (g_nf, 0, 2 * width)])
    end_bucket.start_share()
    if fused:
        mid_bucket.finish([(g_es, 0, width), (g_ef, 0, width)])
        end_bucket.finish([(g_ef, width, 2 * width)])


def write_out(*refs):
    sems = refs[-1]
    half = len(refs) // 2
    copies = [
        pltpu.make_async_copy(refs[i], refs[half + i], sems.at[i]) for i in range(half)
    ]
    for copy in copies:
        copy.start()
    for copy in copies:
        copy.wait()


def local(sizes, nodes, edges, edge_ends, edge_count, send_rows, cotangent, ef, es, nf, ns):
    fused, patches, reps, group = sizes
    verts, width = nodes.shape[1:]
    slots = edges.shape[1]
    hops, slot = send_rows.shape
    seam = hops * slot
    table = verts + -(-seam // LANES) * LANES
    rows = ef.shape[0] + es.shape[0] + nf.shape[0] + ns.shape[0]
    vmem = pl.BlockSpec(memory_space=pltpu.VMEM)
    smem = pl.BlockSpec(memory_space=pltpu.SMEM)
    hbm = pl.BlockSpec(memory_space=pltpu.HBM)

    def like(shape, kind=BF16):
        return jax.ShapeDtypeStruct(shape, kind)

    outs = [like((verts, width)), like((verts, width)), like((slots, width))]
    if fused:
        outs += [like(ef.shape), like(es.shape), like(nf.shape), like(ns.shape)]
    else:
        outs += [like((rows, width), F32)]
    scratch = [pltpu.VMEM((rows, width), F32)] if fused else []
    scratch += [
        pltpu.VMEM((2, slots, LANES), jnp.int32),
        pltpu.VMEM((seam, verts), BF16),
        pltpu.VMEM((verts, width), BF16),
        pltpu.VMEM((table, width), BF16),
        pltpu.VMEM((slots, width), F32),
        pltpu.VMEM((slots, width), F32),
        pltpu.VMEM((slots, 1), F32),
        pltpu.VMEM((slots, width), BF16),
        pltpu.VMEM((slots, width), BF16),
        pltpu.VMEM((4, hops, slot, width), BF16),
        pltpu.VMEM((4, hops, slot, width), BF16),
        pltpu.VMEM((verts, width), F32),
        pltpu.VMEM((verts, width), F32),
        pltpu.VMEM((verts, width), BF16),
        pltpu.VMEM((verts, width), BF16),
        pltpu.VMEM((verts, width), BF16),
        pltpu.VMEM((table, width), BF16),
        pltpu.VMEM((verts, width), BF16),
        pltpu.VMEM((verts, width), F32),
        pltpu.SemaphoreType.DMA((4, hops)),
        pltpu.SemaphoreType.DMA((4, hops)),
        pltpu.VMEM((slots, width), F32),
    ]
    held = (nodes[0], edges[0], edge_ends.T, send_rows, cotangent[0], ef, es, nf, ns)
    held = tuple(pltpu.with_memory_space_constraint(x, pltpu.HBM) for x in held)
    scratch += [pltpu.VMEM(x.shape, x.dtype) for x in held]
    scratch += [pltpu.SemaphoreType.DMA((len(held),))]
    if fused:
        scratch += [pltpu.VMEM((rows // PACK, PACK, LANES), BF16)] * 6
        quad, lines = INNER * reps // 2, patches // INNER
        scratch += [pltpu.VMEM((rows // PACK * lines // quad, PACK, LANES), BF16)]
        scratch += [pltpu.SemaphoreType.DMA((3, 5, max(quad, lines)))] * 2
    got = pl.pallas_call(
        functools.partial(body, sizes),
        out_shape=outs,
        in_specs=[hbm] * 3 + [smem] + [hbm] * 6,
        out_specs=[vmem] * len(outs),
        scratch_shapes=scratch,
        compiler_params=pltpu.CompilerParams(
            collective_id=0, has_side_effects=True, vmem_limit_bytes=48 * 2**20
        ),
        name="message_layer",
    )(*held[:3], edge_count, *held[3:])
    got = pl.pallas_call(
        write_out,
        out_shape=outs,
        in_specs=[vmem] * len(outs),
        out_specs=[hbm] * len(outs),
        scratch_shapes=[pltpu.SemaphoreType.DMA((len(outs),))],
        compiler_params=pltpu.CompilerParams(vmem_limit_bytes=2**20),
        name="write_out",
    )(*got)
    new_nodes, g_nodes, g_edges = got[:3]
    if fused:
        g_ef, g_es, g_nf, g_ns = got[3:]
    else:
        total = lax.psum(got[3], ("patch", "rep")).astype(BF16)
        g_ns = total[:width]
        g_nf = total[width : 3 * width]
        g_es = total[3 * width : 4 * width]
        g_ef = total[4 * width :]
    return new_nodes[None], g_nodes[None], g_edges[None], g_ef, g_es, g_nf, g_ns


def solution(mesh):
    patches, reps = mesh.shape["patch"], mesh.shape["rep"]
    group = patches * reps // 2
    fused = reps % 2 == 0 and patches % INNER == 0 and (2 * LANES) % (PACK * group) == 0
    sizes = (fused, patches, reps, group)
    rows = P("rep", "patch", None)
    placed = (rows, rows, P("patch", None), P("patch"), P("patch", None), rows, P(), P(), P(), P())
    return jax.shard_map(
        functools.partial(local, sizes),
        mesh=mesh,
        in_specs=placed,
        out_specs=(rows, rows, rows, P(), P(), P(), P()),
        check_vma=False,
    )
```
